256 devices in a mesh: seq: 8 (over y, core), batch: 32 (over x, z).
Axes of the slice: x: 4, y: 4, z: 8, core: 2. Of those that a mesh axis runs over, the one named last changes fastest.
Arguments:
- hidden: bfloat16 [32, 3072, 1024], P('batch', 'seq'), may hold values from -6 to 6
- grad_out: bfloat16 [32, 3072, 1024], P('batch', 'seq'), may hold values from -6 to 6
- block_offsets: int32 [32, 16, 24, 4], P('batch', 'seq'), may hold values from 0 to 23, as said below
- w_query: bfloat16 [1024, 1024], replicated, may hold values from -0.1875 to 0.1875
- w_key: bfloat16 [1024, 1024], replicated, may hold values from -0.1875 to 0.1875
- w_value: bfloat16 [1024, 1024], replicated, may hold values from -0.1875 to 0.1875
- w_out: bfloat16 [1024, 1024], replicated, may hold values from -0.1875 to 0.1875
Outputs:
- grad_hidden: bfloat16 [32, 3072, 1024], P('batch', 'seq')
- grad_weights: float32 [4, 1024, 1024], P(None, 'batch', 'seq')
The draws below stay inside these ranges and needn't reach their ends.
Inputs may be any that keep to these rules, and one draw needn't show every extreme that they name: `block_offsets`: slot 0 of every list is 0 (the query's own block); the other slots of a list hold distinct values from 1 to 23, and a value greater than the query block's index leaves its slot empty.
All inputs are finite; a program needn't handle non-finite values.
Results may differ from the reference program's by a relative error of at most 0.012.
Values may be sent and summed in bfloat16 or wider, within the bound.
A program may use at most 128 MiB of HBM per device.

```python
import math
import jax
import jax.numpy as jnp
from jax import lax

D = 1024
H = 16
HD = 64
BLK = 128
NSEL = 4
SEQ_LEN = 3072
QB = 24
NCHUNK = 32


def draw_hidden(key, part):
    base = jax.random.normal(jax.random.fold_in(key, 11), (NCHUNK, SEQ_LEN, D), jnp.float32)
    base = jnp.clip(base, -6.0, 6.0)
    return base.astype(jnp.bfloat16)


def draw_block_offsets(key, part):
    ranks = jax.random.randint(jax.random.fold_in(key, 21), (NCHUNK, H, QB, QB - 1), 0, 1 << 20, dtype=jnp.int32)
    ranks = ranks * (QB - 1) + jnp.arange(QB - 1, dtype=jnp.int32)
    order = jnp.argsort(ranks, axis=-1, stable=True)[..., :NSEL - 1].astype(jnp.int32) + 1
    own_block = jnp.zeros((NCHUNK, H, QB, 1), jnp.int32)
    return jnp.concatenate([own_block, order], axis=-1)


def steps_of(stream_key, dims, cuts, smallest, largest):
    gain, own = 1.0, jax.random.fold_in(stream_key, 6)
    for axis_at, blocks in cuts:
        heights = jnp.exp(jax.random.uniform(jax.random.fold_in(own, axis_at), (blocks,), jnp.float32, smallest / len(cuts), largest / len(cuts)))
        gain = gain * jnp.repeat(heights, dims[axis_at] // blocks).reshape([-1 if axis == axis_at else 1 for axis in range(len(dims))])
    return gain


def noise(stream_key, dims, deviation, reach, split=(), held_as=jnp.bfloat16):
    gain = steps_of(stream_key, dims, split, -0.22, 0.18) if split else 1.0
    result = jax.random.normal(stream_key, dims, jnp.float32) * deviation * gain
    return jnp.minimum(jnp.maximum(result, -reach), reach).astype(held_as)


def setup_inputs(seed: int = 0) -> dict:
    key_list = jax.random.split(jax.random.key(seed), 8)
    hidden = draw_hidden(jax.random.fold_in(key_list[7], 71), 0)
    grad_out = noise(key_list[1], (NCHUNK, SEQ_LEN, D), 1.0, 6.0, ((0, 32), (1, 8)))
    block_offsets = draw_block_offsets(jax.random.fold_in(key_list[7], 71), 0)
    w_query = noise(key_list[3], (D, D), D ** -0.5, 0.1875)
    w_key = noise(key_list[4], (D, D), D ** -0.5, 0.1875)
    w_value = noise(key_list[5], (D, D), D ** -0.5, 0.1875)
    w_out = noise(key_list[6], (D, D), D ** -0.5, 0.1875)
    return dict(hidden=hidden, grad_out=grad_out, block_offsets=block_offsets, w_query=w_query, w_key=w_key, w_value=w_value, w_out=w_out)


def pick_blocks(source, chosen):
    return source[chosen]

def add_blocks(running, chosen, portion):
    return running.at[chosen].add(portion)

def scatter_blocks(running, block_ids, portion):
    heads_n = portion.shape[0]
    flat_ids = block_ids.reshape(heads_n, -1)
    flat_part = portion.reshape((heads_n, -1) + portion.shape[3:])
    return jax.vmap(add_blocks)(running, flat_ids, flat_part)

def attend_group(queries, key_all, value_all, out_grads, offsets, first_block):
    group_len = queries.shape[1]
    block_len = queries.shape[2]
    score_scale = 1.0 / math.sqrt(queries.shape[3])
    query_block = first_block + jnp.arange(group_len, dtype=jnp.int32)
    usable = offsets <= query_block[None, :, None]
    block_ids = jnp.where(usable, query_block[None, :, None] - offsets, 0).astype(jnp.int32)
    picked_keys = jax.vmap(pick_blocks)(key_all, block_ids)
    picked_values = jax.vmap(pick_blocks)(value_all, block_ids)
    scores = jnp.einsum('hgqd,hgnkd->hgqnk', queries.astype(jnp.float32), picked_keys.astype(jnp.float32)) * score_scale
    within = jnp.arange(block_len, dtype=jnp.int32)
    query_pos = query_block[:, None] * block_len + within[None, :]
    key_pos = block_ids[..., None] * block_len + within
    allowed = usable[:, :, None, :, None] & (key_pos[:, :, None, :, :] <= query_pos[None, :, :, None, None])
    row_top = lax.optimization_barrier(jnp.max(jnp.where(allowed, scores, -jnp.inf), axis=(3, 4), keepdims=True))
    raised = jnp.where(allowed, jnp.exp(scores - row_top), 0.0)
    denom_sum = lax.optimization_barrier(jnp.sum(raised, axis=(3, 4), keepdims=True))
    probabilities = raised / denom_sum
    probs_half = probabilities.astype(jnp.bfloat16)
    attended = jnp.einsum('hgqnk,hgnkd->hgqd', probs_half.astype(jnp.float32), picked_values.astype(jnp.float32)).astype(jnp.bfloat16)
    delta_rows = lax.optimization_barrier(jnp.sum(out_grads.astype(jnp.float32) * attended.astype(jnp.float32), axis=-1))
    prob_grad = jnp.einsum('hgqd,hgnkd->hgqnk', out_grads.astype(jnp.float32), picked_values.astype(jnp.float32))
    score_grad = (probabilities * (prob_grad - delta_rows[:, :, :, None, None])).astype(jnp.bfloat16)
    query_grad = (jnp.einsum('hgqnk,hgnkd->hgqd', score_grad.astype(jnp.float32), picked_keys.astype(jnp.float32)) * score_scale).astype(jnp.bfloat16)
    key_part = jnp.einsum('hgqnk,hgqd->hgnkd', score_grad.astype(jnp.float32), queries.astype(jnp.float32)) * score_scale
    value_part = jnp.einsum('hgqnk,hgqd->hgnkd', probs_half.astype(jnp.float32), out_grads.astype(jnp.float32))
    return (attended, query_grad, key_part, value_part, block_ids)

def heads_first(matrix):
    return matrix.reshape(QB, BLK, H, HD).transpose(2, 0, 1, 3)

def tokens_first(blocks):
    return blocks.transpose(1, 2, 0, 3).reshape(SEQ_LEN, H * HD)

def reference(hidden, grad_out, block_offsets, w_query, w_key, w_value, w_out):

    def one_stretch(running, inputs):
        tokens, grad_rows, offsets = inputs
        queries = jnp.dot(tokens, w_query, preferred_element_type=jnp.float32).astype(jnp.bfloat16)
        key_rows = jnp.dot(tokens, w_key, preferred_element_type=jnp.float32).astype(jnp.bfloat16)
        value_rows = jnp.dot(tokens, w_value, preferred_element_type=jnp.float32).astype(jnp.bfloat16)
        attn_grad = jnp.dot(grad_rows, w_out.T, preferred_element_type=jnp.float32).astype(jnp.bfloat16)
        attended, query_grad, key_part, value_part, block_ids = attend_group(heads_first(queries), heads_first(key_rows), heads_first(value_rows), heads_first(attn_grad), offsets, jnp.int32(0))
        empty = jnp.zeros((H, QB, BLK, HD), jnp.float32)
        key_grad = scatter_blocks(empty, block_ids, key_part).astype(jnp.bfloat16)
        value_grad = scatter_blocks(empty, block_ids, value_part).astype(jnp.bfloat16)
        query_tok = tokens_first(query_grad)
        key_tok = tokens_first(key_grad)
        value_tok = tokens_first(value_grad)
        attended_tok = tokens_first(attended)
        grad_hidden = (jnp.dot(query_tok, w_query.T, preferred_element_type=jnp.float32) + jnp.dot(key_tok, w_key.T, preferred_element_type=jnp.float32) + jnp.dot(value_tok, w_value.T, preferred_element_type=jnp.float32)).astype(jnp.bfloat16)
        term_rows = jnp.stack([jnp.dot(tokens.T, query_tok, preferred_element_type=jnp.float32), jnp.dot(tokens.T, key_tok, preferred_element_type=jnp.float32), jnp.dot(tokens.T, value_tok, preferred_element_type=jnp.float32), jnp.dot(attended_tok.T, grad_rows, preferred_element_type=jnp.float32)])
        return (running + term_rows, grad_hidden)
    summed, grad_hidden = lax.scan(one_stretch, jnp.zeros((4, D, D), jnp.float32), (hidden, grad_out, block_offsets))
    return (grad_hidden, summed * (1.0 / math.sqrt(NCHUNK * SEQ_LEN)))
```

```python
import functools
import math

import jax
import jax.numpy as jnp
from jax import lax
from jax.experimental import pallas as pl
from jax.experimental.pallas import tpu as pltpu
from jax.sharding import Mesh
from jax.sharding import PartitionSpec as P


BLK = 128
HEADS = 2
HD = 64
NT = (((1,), (1,)), ((), ()))


def dot(a, b):
    return jnp.dot(a, b, preferred_element_type=jnp.float32)


def dot_nt(a, b):
    return lax.dot_general(a, b, NT, preferred_element_type=jnp.float32)


def attend_head(head, block, listed, q, k, v, do, kt, vt, dot_, key_acc, value_acc, flipped):
    lanes = lax.broadcasted_iota(jnp.int32, (BLK, BLK), 1)
    mine = (lanes >= HD) if head else (lanes < HD)
    rows = pl.ds(head * HD, HD)
    own = pl.ds(pl.multiple_of(block * BLK, BLK), BLK)
    starts = [pl.ds(pl.multiple_of(n * BLK, BLK), BLK) for n in listed]
    query = jnp.where(mine, q[own, :], jnp.zeros((), jnp.bfloat16))
    grad = jnp.where(mine, do[own, :], jnp.zeros((), jnp.bfloat16))
    scores = [dot_nt(k[s, :], query) for s in starts]
    key_at = lax.broadcasted_iota(jnp.int32, (BLK, BLK), 0)
    scores[0] = jnp.where(key_at <= lanes, scores[0], -jnp.inf)
    prob_grad = [dot_nt(v[s, :], grad) for s in starts]
    top = scores[0]
    for s in scores[1:]:
        top = jnp.maximum(top, s)
    top = jnp.max(top, axis=0, keepdims=True)
    raised = [jnp.exp((s - top) * (1.0 / 8.0)) for s in scores]
    total = raised[0]
    for e in raised[1:]:
        total = total + e
    share = 1.0 / jnp.sum(total, axis=0, keepdims=True)
    probs = [e * share for e in raised]
    halves = [p.astype(jnp.bfloat16) for p in probs]
    stacked = jnp.concatenate(halves, axis=0)
    attended = dot(jnp.concatenate([vt[n, rows, :] for n in listed], axis=1), stacked)
    attended = attended.astype(jnp.bfloat16)
    delta = jnp.sum(
        dot_[block, rows, :].astype(jnp.float32) * attended.astype(jnp.float32), axis=0, keepdims=True
    )
    score_grads = [
        (p * (g - delta)).astype(jnp.bfloat16) for p, g in zip(probs, prob_grad)
    ]
    graded = jnp.concatenate(score_grads, axis=0)
    query_grad = dot(jnp.concatenate([kt[n, rows, :] for n in listed], axis=1), graded)
    flipped[0, block, rows, :] = (query_grad * (1.0 / 8.0)).astype(jnp.bfloat16)
    flipped[3, block, rows, :] = attended
    value_part = dot(stacked, grad)
    key_part = dot(graded, query)
    for i, s in enumerate(starts):
        value_acc[s, :] += value_part[i * BLK : (i + 1) * BLK]
        key_acc[s, :] += key_part[i * BLK : (i + 1) * BLK]


def attention_kernel(offs, heads, turned, grads, flipped, key_acc, value_acc):
    q, k, v, do = (heads.at[n] for n in range(4))
    kt, vt, dot_ = (turned.at[n] for n in range(3))
    blocks = heads.shape[1] // BLK
    key_acc[...] = jnp.zeros_like(key_acc)
    value_acc[...] = jnp.zeros_like(value_acc)

    @pl.loop(0, blocks)
    def _(block):
        for head in range(HEADS):
            o1 = offs[head, block * 4 + 1]
            o2 = offs[head, block * 4 + 2]
            o3 = offs[head, block * 4 + 3]
            v1 = (o1 <= block).astype(jnp.int32)
            v2 = (o2 <= block).astype(jnp.int32)
            v3 = (o3 <= block).astype(jnp.int32)
            count = v1 + v2 + v3
            first = jnp.where(v1 == 1, o1, jnp.where(v2 == 1, o2, o3))
            second = jnp.where(v1 + v2 == 2, o2, o3)
            for extra in range(4):
                picked = [block] + [
                    jnp.maximum(block - o, 0) for o in (first, second, o3)[:extra]
                ]

                @pl.when(count == extra)
                def _(picked=picked, head=head):
                    attend_head(
                        head, block, picked, q, k, v, do, kt, vt, dot_, key_acc, value_acc, flipped
                    )

    @pl.loop(0, blocks)
    def _(block):
        own = pl.ds(pl.multiple_of(block * BLK, BLK), BLK)
        grads[0, own, :] = flipped[0, block].T
        kg = (key_acc[own, :] * (1.0 / 8.0)).astype(jnp.bfloat16)
        vg = value_acc[own, :].astype(jnp.bfloat16)
        grads[1, own, :] = kg
        grads[2, own, :] = vg
        flipped[1, block] = kg.T
        flipped[2, block] = vg.T


def attention(offsets, heads, turned):
    length, width = heads.shape[1:]
    blocks = length // BLK
    whole = pl.BlockSpec(memory_space=pltpu.VMEM)
    return pl.pallas_call(
        attention_kernel,
        out_shape=(
            jax.ShapeDtypeStruct((3, length, width), jnp.bfloat16),
            jax.ShapeDtypeStruct((4, blocks, width, BLK), jnp.bfloat16),
        ),
        in_specs=[pl.BlockSpec(memory_space=pltpu.SMEM)] + [whole] * 2,
        out_specs=(whole, whole),
        scratch_shapes=[
            pltpu.VMEM((length, width), jnp.float32),
            pltpu.VMEM((length, width), jnp.float32),
        ],
        compiler_params=pltpu.CompilerParams(vmem_limit_bytes=48 << 20),
        cost_estimate=pl.CostEstimate(flops=4 << 30, bytes_accessed=12 << 20, transcendentals=3 << 20),
        name="attention",
    )(offsets.reshape(HEADS, -1), heads, turned)


ROWS = 384
HALF = 192
WIDTH = 128
D = 1024
CHUNKS = 8


def remote(src, dst, send, recv, **where):
    return pltpu.make_async_remote_copy(
        src_ref=src, dst_ref=dst, send_sem=send, recv_sem=recv,
        device_id=where, device_id_type=pl.DeviceIdType.MESH,
    )


def gather_kernel(
    hidden, grad_out, w_query, w_key, w_value, w_out, rows_all, heads, flipped,
    land, w_in, w_back, heads_v, flipped_v, send, recv, load, save,
):
    y, c = lax.axis_index("seq_0"), lax.axis_index("seq_1")
    right, left, opposite = (y + 1) % 4, (y + 3) % 4, (y + 2) % 4
    own = 2 * y + c
    to_right = dict(seq_0=right, seq_1=c)
    to_left = dict(seq_0=left, seq_1=c)
    to_mate = dict(seq_0=y, seq_1=1 - c)
    upper, lower = pl.ds(0, HALF), pl.ds(HALF, HALF)
    both = pl.ds(0, ROWS)
    sources = (hidden, grad_out)

    barrier = pltpu.get_barrier_semaphore()
    for peer in (to_right, to_left, to_mate):
        pl.semaphore_signal(barrier, inc=1, device_id=peer, device_id_type=pl.DeviceIdType.MESH)
    pl.semaphore_wait(barrier, 3)

    def place(a, chunk, part):
        return land.at[a, chunk, part]

    def copy(a, slot, chunk, part, where, src=None):
        at = place(a, chunk, part)
        return remote(at if src is None else src, at, send.at[a, slot], recv.at[a, slot], **where)

    def arrived(a, slot, chunk, part):
        copy(a, slot, chunk, part, to_mate).wait_recv()

    def start_own(a):
        src = sources[a]
        copy(a, 0, own, upper, to_right, src.at[upper]).start()
        copy(a, 3, own, lower, to_left, src.at[lower]).start()
        copy(a, 1, own, lower, to_right, src.at[lower]).start()
        copy(a, 4, own, upper, to_left, src.at[upper]).start()
        copy(a, 6, own, both, to_mate, src).start()

    def relay_near(a):
        arrived(a, 0, 2 * left + c, upper)
        copy(a, 2, 2 * left + c, upper, to_right).start()
        copy(a, 7, 2 * left + c, upper, to_mate).start()
        arrived(a, 3, 2 * right + c, lower)
        copy(a, 5, 2 * right + c, lower, to_left).start()
        copy(a, 9, 2 * right + c, lower, to_mate).start()

    def relay_rest(a):
        arrived(a, 1, 2 * left + c, lower)
        copy(a, 8, 2 * left + c, lower, to_mate).start()
        arrived(a, 4, 2 * right + c, upper)
        copy(a, 10, 2 * right + c, upper, to_mate).start()

    def relay_far(a):
        arrived(a, 2, 2 * opposite + c, upper)
        copy(a, 11, 2 * opposite + c, upper, to_mate).start()
        arrived(a, 5, 2 * opposite + c, lower)
        copy(a, 12, 2 * opposite + c, lower, to_mate).start()

    def project(a, count, chip_of):
        @pl.loop(0, count)
        def _(j):
            chunk = 2 * chip_of(j // 2) + j % 2
            pltpu.make_async_copy(land.at[a, chunk], rows_all.at[a, chunk], save.at[a]).start()
            at = pl.ds(pl.multiple_of(chunk * ROWS, ROWS), ROWS)
            x = land[a, chunk]
            if a == 0:
                for n in range(3):
                    part = dot(x, w_in[n]).astype(jnp.bfloat16)
                    heads_v[n, at, :] = part
                    if n > 0:
                        for i in range(3):
                            flipped_v[n - 1, chunk * 3 + i] = part[i * BLK : (i + 1) * BLK].T
            else:
                part = dot_nt(x, w_back[...]).astype(jnp.bfloat16)
                heads_v[3, at, :] = part
                for i in range(3):
                    flipped_v[2, chunk * 3 + i] = part[i * BLK : (i + 1) * BLK].T

    mine = pl.ds(pl.multiple_of(own * WIDTH, WIDTH), WIDTH)
    start_own(0)
    loads = [
        pltpu.make_async_copy(hidden, land.at[0, own], load.at[0]),
        pltpu.make_async_copy(w_query.at[:, mine], w_in.at[0], load.at[1]),
        pltpu.make_async_copy(w_key.at[:, mine], w_in.at[1], load.at[2]),
        pltpu.make_async_copy(w_value.at[:, mine], w_in.at[2], load.at[3]),
        pltpu.make_async_copy(grad_out, land.at[1, own], load.at[4]),
        pltpu.make_async_copy(w_out.at[mine, :], w_back, load.at[5]),
    ]
    for item in loads:
        item.start()
    relay_near(0)
    start_own(1)
    for item in loads:
        item.wait()
    for a in range(2):
        if a == 1:
            relay_near(1)
        arrived(a, 6, 2 * y + 1 - c, both)
        project(a, 2, lambda i: y)
        relay_rest(a)
        arrived(a, 7, 2 * left + 1 - c, upper)
        arrived(a, 9, 2 * right + 1 - c, lower)
        arrived(a, 8, 2 * left + 1 - c, lower)
        arrived(a, 10, 2 * right + 1 - c, upper)
        project(a, 4, lambda i: (y + 1 + 2 * i) % 4)
        relay_far(a)
        arrived(a, 11, 2 * opposite + 1 - c, upper)
        arrived(a, 12, 2 * opposite + 1 - c, lower)
        project(a, 2, lambda i: opposite)
        first = 0 if a == 0 else 3
        count = 3 if a == 0 else 1
        pltpu.make_async_copy(
            heads_v.at[pl.ds(first, count)], heads.at[pl.ds(first, count)], save.at[2 + a]
        ).start()
        first, count = (0, 2) if a == 0 else (2, 1)
        pltpu.make_async_copy(
            flipped_v.at[pl.ds(first, count)], flipped.at[pl.ds(first, count)], save.at[4 + a]
        ).start()
    for a in range(2):
        pltpu.make_async_copy(land.at[a], rows_all.at[a], save.at[a]).wait()
        first, count = (0, 3) if a == 0 else (3, 1)
        pltpu.make_async_copy(
            heads_v.at[pl.ds(first, count)], heads.at[pl.ds(first, count)], save.at[2 + a]
        ).wait()
        first, count = (0, 2) if a == 0 else (2, 1)
        pltpu.make_async_copy(
            flipped_v.at[pl.ds(first, count)], flipped.at[pl.ds(first, count)], save.at[4 + a]
        ).wait()
        for slot, chunk, part in (
            (0, own, upper), (1, own, lower), (2, 2 * left + c, upper),
            (3, own, lower), (4, own, upper), (5, 2 * right + c, lower),
            (6, own, both), (7, 2 * left + c, upper), (8, 2 * left + c, lower),
            (9, 2 * right + c, lower), (10, 2 * right + c, upper),
            (11, 2 * opposite + c, upper), (12, 2 * opposite + c, lower),
        ):
            copy(a, slot, chunk, part, to_mate).wait_send()


def gather(hidden, grad_out, w_query, w_key, w_value, w_out):
    anywhere = pl.BlockSpec(memory_space=pl.ANY)
    length = CHUNKS * ROWS
    blocks = length // BLK
    bf16 = jnp.bfloat16
    return pl.pallas_call(
        gather_kernel,
        out_shape=(
            jax.ShapeDtypeStruct((2, CHUNKS, ROWS, D), bf16),
            jax.ShapeDtypeStruct((4, length, WIDTH), bf16),
            jax.ShapeDtypeStruct((3, blocks, BLK, BLK), bf16),
        ),
        in_specs=[anywhere] * 6,
        out_specs=(anywhere,) * 3,
        scratch_shapes=[
            pltpu.VMEM((2, CHUNKS, ROWS, D), bf16),
            pltpu.VMEM((3, D, WIDTH), bf16),
            pltpu.VMEM((WIDTH, D), bf16),
            pltpu.VMEM((4, length, WIDTH), bf16),
            pltpu.VMEM((3, blocks, BLK, BLK), bf16),
            pltpu.SemaphoreType.DMA((2, 13)),
            pltpu.SemaphoreType.DMA((2, 13)),
            pltpu.SemaphoreType.DMA((6,)),
            pltpu.SemaphoreType.DMA((6,)),
        ],
        compiler_params=pltpu.CompilerParams(
            collective_id=0, has_side_effects=True, vmem_limit_bytes=60 << 20
        ),
        name="gather_and_project",
    )(hidden, grad_out, w_query, w_key, w_value, w_out)


SHIFTS = ((0, 1), (1, 0), (1, 1), (3, 0), (3, 1), (2, 0), (2, 1))


def return_kernel(
    norm, rows_all, grads, flipped, w_query, w_key, w_value, grad_hidden, grad_weights,
    rows_v, flipped_v, w_v, back, out_acc, back_part, part_acc, part, x_in, z_out, z_in,
    y_send, y_recv, o_send, o_recv, x_send, x_recv, z_send, z_recv, load,
):
    y, c = lax.axis_index("seq_0"), lax.axis_index("seq_1")
    x, z = lax.axis_index("batch_0"), lax.axis_index("batch_1")
    own = 2 * y + c
    peers = [dict(seq_0=(y + dy) % 4, seq_1=(c + dc) % 2) for dy, dc in SHIFTS]
    x_peers = [(x + i) % 4 for i in (1, 3, 2)]
    z_peers = [(z + i) % 8 for i in (1, 7, 2, 6, 3, 5, 4)]

    barrier = pltpu.get_barrier_semaphore()
    everyone = peers + [dict(batch_0=p) for p in x_peers] + [dict(batch_1=p) for p in z_peers]
    for peer in everyone:
        pl.semaphore_signal(barrier, inc=1, device_id=peer, device_id_type=pl.DeviceIdType.MESH)
    pl.semaphore_wait(barrier, len(everyone))

    def chunk_of(peer):
        return 2 * peer["seq_0"] + peer["seq_1"]

    def lanes(chunk):
        return pl.ds(pl.multiple_of(chunk * WIDTH, WIDTH), WIDTH)

    def rows(chunk):
        return pl.ds(pl.multiple_of(chunk * ROWS, ROWS), ROWS)

    def y_copy(a, i):
        peer = peers[i]
        return remote(
            grads.at[a, rows(chunk_of(peer))], back.at[a, :, lanes(own)],
            y_send.at[a, i], y_recv.at[a, own], **peer,
        )

    def y_wait(a, chunk):
        pltpu.make_async_remote_copy(
            src_ref=grads.at[a, rows(chunk)], dst_ref=back.at[a, :, lanes(chunk)],
            send_sem=y_send.at[a, 0], recv_sem=y_recv.at[a, chunk],
            device_id=peers[0], device_id_type=pl.DeviceIdType.MESH,
        ).wait_recv()

    loads = [
        pltpu.make_async_copy(rows_all.at[1], rows_v.at[1], load.at[0]),
        pltpu.make_async_copy(flipped, flipped_v, load.at[1]),
        pltpu.make_async_copy(rows_all.at[0], rows_v.at[0], load.at[2]),
        pltpu.make_async_copy(w_query, w_v.at[0], load.at[3]),
        pltpu.make_async_copy(w_key, w_v.at[1], load.at[4]),
        pltpu.make_async_copy(w_value, w_v.at[2], load.at[5]),
    ] + [
        pltpu.make_async_copy(grads.at[a, rows(own)], back.at[a, :, lanes(own)], load.at[6 + a])
        for a in range(3)
    ]
    for item in loads[:2]:
        item.start()
    for i in range(7):
        y_copy(2, i).start()
    for item in loads[2:]:
        item.start()

    def side_by_side(a, j):
        return jnp.concatenate([flipped_v[a, 3 * j + i] for i in range(3)], axis=1)

    loads[0].wait()
    loads[1].wait()
    part_acc[0:WIDTH] = dot(side_by_side(3, 0), rows_v[1, 0])

    @pl.loop(1, CHUNKS)
    def _(j):
        part_acc[0:WIDTH] += dot(side_by_side(3, j), rows_v[1, j])

    back_part[...] = part_acc[0:WIDTH].astype(jnp.bfloat16)

    def o_copy(i):
        peer = peers[i]
        return remote(
            back_part.at[:, lanes(chunk_of(peer))], part.at[3, lanes(own)],
            o_send.at[i], o_recv.at[own], **peer,
        )

    def o_wait(chunk):
        pltpu.make_async_remote_copy(
            src_ref=back_part.at[:, lanes(chunk)], dst_ref=part.at[3, lanes(chunk)],
            send_sem=o_send.at[0], recv_sem=o_recv.at[chunk],
            device_id=peers[0], device_id_type=pl.DeviceIdType.MESH,
        ).wait_recv()

    for i in range(7):
        o_copy(i).start()
    for a in (1, 0):
        for i in range(7):
            y_copy(a, i).start()
    part[3, lanes(own), :] = back_part[:, lanes(own)]

    loads[2].wait()

    def three(j):
        return jnp.concatenate([side_by_side(a, j) for a in range(3)], axis=0)

    part_acc[...] = dot(three(0), rows_v[0, 0])

    @pl.loop(1, CHUNKS)
    def _(j):
        part_acc[...] += dot(three(j), rows_v[0, j])

    @pl.loop(0, 8)
    def _(t):
        for a in range(3):
            tile = part_acc[pl.ds(a * WIDTH, WIDTH), lanes(t)]
            part[a, lanes(t), :] = tile.T.astype(jnp.bfloat16)

    quarter = D // 4

    def x_copy(k, i):
        p = x_peers[i]
        which = pl.ds(0, 3) if k == 0 else pl.ds(3, 1)
        return remote(
            part.at[which, pl.ds(pl.multiple_of(p * quarter, quarter), quarter)],
            x_in.at[x, which], x_send.at[k, i], x_recv.at[k, x], batch_0=p,
        )

    def x_wait(k, p):
        which = pl.ds(0, 3) if k == 0 else pl.ds(3, 1)
        pltpu.make_async_remote_copy(
            src_ref=x_in.at[p, which], dst_ref=x_in.at[p, which],
            send_sem=x_send.at[k, 0], recv_sem=x_recv.at[k, p],
            device_id=dict(batch_0=x_peers[0]), device_id_type=pl.DeviceIdType.MESH,
        ).wait_recv()

    for i in range(3):
        x_copy(0, i).start()
    for item in loads[3:]:
        item.wait()

    def add_chips(count, chip_of, first):
        @pl.loop(0, count)
        def _(j):
            at = pl.ds(pl.multiple_of(chip_of(j) * 2 * WIDTH, 2 * WIDTH), 2 * WIDTH)
            total = dot_nt(back[0, :, at], w_v[0, :, at])
            total += dot_nt(back[1, :, at], w_v[1, :, at])
            total += dot_nt(back[2, :, at], w_v[2, :, at])
            if first:
                out_acc[...] = total
            else:
                out_acc[...] += total

    for a in (2, 1, 0):
        y_wait(a, 2 * y + 1 - c)
    add_chips(1, lambda j: y, True)

    for peer in peers:
        o_wait(chunk_of(peer))
    for i in range(3):
        x_copy(1, i).start()
    for p in x_peers:
        x_wait(0, p)
    for p in x_peers:
        x_wait(1, p)
    total = part[:, pl.ds(pl.multiple_of(x * quarter, quarter), quarter), :].astype(jnp.float32)
    for p in x_peers:
        total += x_in[p].astype(jnp.float32)
    z_out[...] = total.astype(jnp.bfloat16)

    def z_copy(i):
        p = z_peers[i]
        return remote(
            z_out.at[:, pl.ds(pl.multiple_of(p * 32, 32), 32)], z_in.at[z],
            z_send.at[i], z_recv.at[z], batch_1=p,
        )

    def z_wait(p):
        pltpu.make_async_remote_copy(
            src_ref=z_in.at[p], dst_ref=z_in.at[p],
            send_sem=z_send.at[0], recv_sem=z_recv.at[p],
            device_id=dict(batch_1=z_peers[0]), device_id_type=pl.DeviceIdType.MESH,
        ).wait_recv()

    for i in range(7):
        z_copy(i).start()

    for a in (2, 1, 0):
        for peer in peers[1:5]:
            y_wait(a, chunk_of(peer))
    add_chips(2, lambda j: (y + 1 + 2 * j) % 4, False)

    for p in z_peers:
        z_wait(p)
    total = z_out[:, pl.ds(pl.multiple_of(z * 32, 32), 32), :].astype(jnp.float32)
    for p in z_peers:
        total += z_in[p].astype(jnp.float32)
    grad_weights[...] = total * norm

    for a in (2, 1, 0):
        for peer in peers[5:]:
            y_wait(a, chunk_of(peer))
    at = pl.ds(pl.multiple_of(((y + 2) % 4) * 2 * WIDTH, 2 * WIDTH), 2 * WIDTH)
    total = dot_nt(back[0, :, at], w_v[0, :, at])
    total += dot_nt(back[1, :, at], w_v[1, :, at])
    total += dot_nt(back[2, :, at], w_v[2, :, at])
    grad_hidden[...] = (out_acc[...] + total).astype(jnp.bfloat16)

    for i in range(7):
        for a in range(3):
            y_copy(a, i).wait_send()
        o_copy(i).wait_send()
        z_copy(i).wait_send()
    for i in range(3):
        for k in range(2):
            x_copy(k, i).wait_send()


def hand_back(rows_all, grads, flipped, w_query, w_key, w_value, norm):
    anywhere = pl.BlockSpec(memory_space=pl.ANY)
    whole = pl.BlockSpec(memory_space=pltpu.VMEM)
    bf16 = jnp.bfloat16
    f32 = jnp.float32
    blocks = CHUNKS * ROWS // BLK
    dma = pltpu.SemaphoreType.DMA
    return pl.pallas_call(
        functools.partial(return_kernel, norm),
        out_shape=(
            jax.ShapeDtypeStruct((ROWS, D), bf16),
            jax.ShapeDtypeStruct((4, 32, WIDTH), f32),
        ),
        in_specs=[anywhere] * 6,
        out_specs=(whole, whole),
        scratch_shapes=[
            pltpu.VMEM((2, CHUNKS, ROWS, D), bf16),
            pltpu.VMEM((4, blocks, BLK, BLK), bf16),
            pltpu.VMEM((3, D, D), bf16),
            pltpu.VMEM((3, ROWS, D), bf16),
            pltpu.VMEM((ROWS, D), f32),
            pltpu.VMEM((WIDTH, D), bf16),
            pltpu.VMEM((3 * WIDTH, D), f32),
            pltpu.VMEM((4, D, WIDTH), bf16),
            pltpu.VMEM((4, 4, D // 4, WIDTH), bf16),
            pltpu.VMEM((4, D // 4, WIDTH), bf16),
            pltpu.VMEM((8, 4, 32, WIDTH), bf16),
            dma((3, 7)), dma((3, 8)), dma((7,)), dma((8,)),
            dma((2, 3)), dma((2, 4)), dma((7,)), dma((8,)), dma((9,)),
        ],
        compiler_params=pltpu.CompilerParams(
            collective_id=1, has_side_effects=True, vmem_limit_bytes=60 << 20
        ),
        name="return_and_reduce",
    )(rows_all, grads, flipped, w_query, w_key, w_value)


BATCH = ("batch_0", "batch_1")
SEQ = ("seq_0", "seq_1")


def per_device(hidden, grad_out, block_offsets, w_query, w_key, w_value, w_out):
    norm = 1.0 / math.sqrt(ROWS * lax.axis_size(SEQ) * lax.axis_size(BATCH))
    rows_all, heads, turned = gather(hidden[0], grad_out[0], w_query, w_key, w_value, w_out)
    grads, flipped = attention(block_offsets[0], heads, turned)
    grad_hidden, grad_weights = hand_back(
        rows_all, grads, flipped, w_query, w_key, w_value, norm
    )
    return (grad_hidden[None], grad_weights)


def solution(mesh):
    torus = Mesh(mesh.devices.reshape(4, 2, 4, 8), ("seq_0", "seq_1", "batch_0", "batch_1"))
    in_specs = (
        P(BATCH, SEQ, None),
        P(BATCH, SEQ, None),
        P(BATCH, SEQ, None, None),
        P(),
        P(),
        P(),
        P(),
    )
    out_specs = (P(BATCH, SEQ, None), P(None, BATCH, SEQ))
    return jax.shard_map(
        per_device, mesh=torus, in_specs=in_specs, out_specs=out_specs, check_vma=False
    )
```

```python
import functools
import math

import jax
import jax.numpy as jnp
from jax import lax
from jax.experimental import pallas as pl
from jax.experimental.pallas import tpu as pltpu
from jax.sharding import Mesh
from jax.sharding import PartitionSpec as P


BLK = 128
HEADS = 2
HD = 64
GROUP = 3
PIECES = 4
NT = (((1,), (1,)), ((), ()))


def dot(a, b):
    return jnp.dot(a, b, preferred_element_type=jnp.float32)


def dot_nt(a, b):
    return lax.dot_general(a, b, NT, preferred_element_type=jnp.float32)


def rows_of(block):
    return pl.ds(pl.multiple_of(block * BLK, BLK), BLK)


def slots_of(offs, head, block):
    o1, o2, o3 = (offs[head, block * 4 + i] for i in (1, 2, 3))
    v1, v2, v3 = ((o <= block).astype(jnp.int32) for o in (o1, o2, o3))
    first = jnp.where(v1 == 1, o1, jnp.where(v2 == 1, o2, o3))
    second = jnp.where(v1 + v2 == 2, o2, o3)
    return v1 + v2 + v3, (first, second, o3)


def attend(jobs, width, blocks, q, k, v, do, kt, vt, acc, flipped):
    lanes = lax.broadcasted_iota(jnp.int32, (BLK, BLK), 1)
    key_at = lax.broadcasted_iota(jnp.int32, (BLK, BLK), 0)
    nothing = jnp.zeros((BLK, BLK), jnp.bfloat16)
    state = []
    for head, block, count, back in jobs:
        listed, used = [block], [None]
        for i in range(1, width):
            listed.append(jnp.maximum(block - back[i - 1], 0))
            used.append(count >= i)
        mine = (lanes >= HD) if head else (lanes < HD)
        query = jnp.where(mine, q[rows_of(block), :], nothing)
        grad = jnp.where(mine, do[rows_of(block), :], nothing)
        both = jnp.concatenate(
            [jnp.concatenate([query, nothing], axis=1), jnp.concatenate([nothing, grad], axis=1)],
            axis=0,
        )
        pairs = jnp.concatenate(
            [jnp.concatenate([grad, nothing], axis=1), jnp.concatenate([nothing, query], axis=1)],
            axis=0,
        )
        state.append(dict(head=head, block=block, listed=listed, used=used, both=both, pairs=pairs))
    for s in state:
        left = jnp.concatenate(
            [
                jnp.concatenate([k[rows_of(n), :] for n in s["listed"]], axis=0),
                jnp.concatenate([v[rows_of(n), :] for n in s["listed"]], axis=0),
            ],
            axis=1,
        )
        r = dot_nt(left, s["both"])
        s["scores"] = [r[i * BLK : (i + 1) * BLK, :BLK] for i in range(width)]
        s["prob_grad"] = [r[i * BLK : (i + 1) * BLK, BLK:] for i in range(width)]
    for s in state:
        scores = s["scores"]
        scores[0] = jnp.where(key_at <= lanes, scores[0], -jnp.inf)
        tops = [jnp.max(x, axis=0, keepdims=True) for x in scores]
        top = tops[0]
        for t, u in zip(tops[1:], s["used"][1:]):
            top = jnp.maximum(top, jnp.where(u, t, -jnp.inf))
        s["shift"] = [
            top if u is None else jnp.where(u, top, jnp.inf) for u in s["used"]
        ]
    for s in state:
        raised = [jnp.exp((x - t) * (1.0 / 8.0)) for x, t in zip(s["scores"], s["shift"])]
        total, weighted = raised[0], raised[0] * s["prob_grad"][0]
        for e, g in zip(raised[1:], s["prob_grad"][1:]):
            total = total + e
            weighted = weighted + e * g
        share = 1.0 / jnp.sum(total, axis=0, keepdims=True)
        delta = jnp.sum(weighted, axis=0, keepdims=True) * share
        probs = [e * share for e in raised]
        s["halves"] = [p.astype(jnp.bfloat16) for p in probs]
        s["graded"] = [
            (p * (g - delta)).astype(jnp.bfloat16) for p, g in zip(probs, s["prob_grad"])
        ]
    for s in state:
        mine = pl.ds(s["head"] * HD, HD)
        attended = dot(
            jnp.concatenate([vt[n, mine, :] for n in s["listed"]], axis=1),
            jnp.concatenate(s["halves"], axis=0),
        )
        query_grad = dot(
            jnp.concatenate([kt[n, mine, :] for n in s["listed"]], axis=1),
            jnp.concatenate(s["graded"], axis=0),
        )
        flipped[0, s["block"], mine, :] = (query_grad * (1.0 / 8.0)).astype(jnp.bfloat16)
        flipped[3, s["block"], mine, :] = attended.astype(jnp.bfloat16)
        left = jnp.concatenate(
            [jnp.concatenate(s["halves"], axis=0), jnp.concatenate(s["graded"], axis=0)], axis=1
        )
        r = dot(left, s["pairs"])
        s["parts"] = [r[i * BLK : (i + 1) * BLK] for i in range(width)]
    for s, t in zip(state[::2], state[1::2]):
        acc[rows_of(s["block"]), :] = s["parts"][0] + t["parts"][0]
    for s in state:
        homes = [
            rows_of(jnp.where(u, n, blocks + i))
            for i, (n, u) in enumerate(zip(s["listed"][1:], s["used"][1:]))
        ]
        sums = [acc[at, :] + part for at, part in zip(homes, s["parts"][1:])]
        for at, new in zip(homes, sums):
            acc[at, :] = new


def attention_kernel(
    offs, heads_h, turned_h, grads_h, flipped_h, heads, turned, grads, flipped, acc, load, save
):
    q, k, v, do = (heads.at[n] for n in range(4))
    kt, vt = (turned.at[n] for n in range(2))
    blocks = turned.shape[1]
    steps = blocks // GROUP
    each = blocks // PIECES

    def loads(piece):
        rows = pl.ds(pl.multiple_of(piece * each * BLK, each * BLK), each * BLK)
        some = pl.ds(piece * each, each)
        return (
            pltpu.make_async_copy(heads_h.at[:, rows], heads.at[:, rows], load.at[0, piece]),
            pltpu.make_async_copy(turned_h.at[:, some], turned.at[:, some], load.at[1, piece]),
        )

    for piece in range(PIECES):
        for item in loads(piece):
            item.start()

    def flipped_out(n, first, count):
        at = pl.ds(first, count)
        return pltpu.make_async_copy(flipped.at[n, at], flipped_h.at[n, at], save.at[n])

    def grads_out(n, first, count):
        at = pl.ds(pl.multiple_of(first * BLK, BLK), count * BLK)
        return pltpu.make_async_copy(grads.at[n, at], grads_h.at[n, at], save.at[4 + n])

    @pl.loop(0, steps)
    def _(step):
        @pl.when(step % (steps // PIECES) == 0)
        def _():
            for item in loads(step // (steps // PIECES)):
                item.wait()

        jobs, most = [], None
        for g in range(GROUP):
            for head in range(HEADS):
                block = step * GROUP + g
                count, back = slots_of(offs, head, block)
                jobs.append((head, block, count, back))
                most = count if most is None else jnp.maximum(most, count)
        for extra in range(4):

            @pl.when(most == extra)
            def _(extra=extra):
                attend(jobs, 1 + extra, blocks, q, k, v, do, kt, vt, acc, flipped)

        for g in range(GROUP):
            block = step * GROUP + g
            grads[0, rows_of(block), :] = flipped[0, block].T
        flipped_out(0, step * GROUP, GROUP).start()
        flipped_out(3, step * GROUP, GROUP).start()
        grads_out(0, step * GROUP, GROUP).start()

    @pl.loop(0, PIECES)
    def _(piece):
        @pl.loop(0, each)
        def _(i):
            block = piece * each + i
            own = rows_of(block)
            both = acc[own, :]
            vg = both[:, :BLK].astype(jnp.bfloat16)
            kg = (both[:, BLK:] * (1.0 / 8.0)).astype(jnp.bfloat16)
            grads[1, own, :] = kg
            grads[2, own, :] = vg
            flipped[1, block] = kg.T
            flipped[2, block] = vg.T

        for n in (1, 2):
            grads_out(n, piece * each, each).start()
            flipped_out(n, piece * each, each).start()

    for n in range(4):
        flipped_out(n, 0, blocks).wait()
    for n in range(3):
        grads_out(n, 0, blocks).wait()


def attention(offsets, heads, turned):
    length, width = heads.shape[1:]
    blocks = length // BLK
    anywhere = pl.BlockSpec(memory_space=pl.ANY)
    bf16 = jnp.bfloat16
    return pl.pallas_call(
        attention_kernel,
        out_shape=(
            jax.ShapeDtypeStruct((3, length, width), bf16),
            jax.ShapeDtypeStruct((4, blocks, width, BLK), bf16),
        ),
        in_specs=[pl.BlockSpec(memory_space=pltpu.SMEM)] + [anywhere] * 2,
        out_specs=(anywhere, anywhere),
        scratch_shapes=[
            pltpu.VMEM((4, length, width), bf16),
            pltpu.VMEM((2, blocks, width, BLK), bf16),
            pltpu.VMEM((3, length, width), bf16),
            pltpu.VMEM((4, blocks, width, BLK), bf16),
            pltpu.VMEM(((blocks + 3) * BLK, 2 * width), jnp.float32),
            pltpu.SemaphoreType.DMA((2, PIECES)),
            pltpu.SemaphoreType.DMA((7,)),
        ],
        compiler_params=pltpu.CompilerParams(vmem_limit_bytes=60 << 20),
        cost_estimate=pl.CostEstimate(flops=4 << 30, bytes_accessed=12 << 20, transcendentals=3 << 20),
        name="attention",
    )(offsets.reshape(HEADS, -1), heads, turned)


ROWS = 384
HALF = 192
WIDTH = 128
D = 1024
CHUNKS = 8


def remote(src, dst, send, recv, **where):
    return pltpu.make_async_remote_copy(
        src_ref=src, dst_ref=dst, send_sem=send, recv_sem=recv,
        device_id=where, device_id_type=pl.DeviceIdType.MESH,
    )


def gather_kernel(
    hidden, grad_out, w_query, w_key, w_value, w_out, rows_all, heads, flipped,
    land, w_in, w_back, heads_v, flipped_v, send, recv, load, save,
):
    y, c = lax.axis_index("seq_0"), lax.axis_index("seq_1")
    right, left, opposite = (y + 1) % 4, (y + 3) % 4, (y + 2) % 4
    own = 2 * y + c
    to_right = dict(seq_0=right, seq_1=c)
    to_left = dict(seq_0=left, seq_1=c)
    to_mate = dict(seq_0=y, seq_1=1 - c)
    upper, lower = pl.ds(0, HALF), pl.ds(HALF, HALF)
    both = pl.ds(0, ROWS)
    sources = (hidden, grad_out)

    barrier = pltpu.get_barrier_semaphore()
    for peer in (to_right, to_left, to_mate):
        pl.semaphore_signal(barrier, inc=1, device_id=peer, device_id_type=pl.DeviceIdType.MESH)
    pl.semaphore_wait(barrier, 3)

    def place(a, chunk, part):
        return land.at[a, chunk, part]

    def copy(a, slot, chunk, part, where, src=None):
        at = place(a, chunk, part)
        return remote(at if src is None else src, at, send.at[a, slot], recv.at[a, slot], **where)

    def arrived(a, slot, chunk, part):
        copy(a, slot, chunk, part, to_mate).wait_recv()

    def start_own(a):
        src = sources[a]
        copy(a, 0, own, upper, to_right, src.at[upper]).start()
        copy(a, 3, own, lower, to_left, src.at[lower]).start()
        copy(a, 1, own, lower, to_right, src.at[lower]).start()
        copy(a, 4, own, upper, to_left, src.at[upper]).start()
        copy(a, 6, own, both, to_mate, src).start()

    def relay_near(a):
        arrived(a, 0, 2 * left + c, upper)
        copy(a, 2, 2 * left + c, upper, to_right).start()
        copy(a, 7, 2 * left + c, upper, to_mate).start()
        arrived(a, 3, 2 * right + c, lower)
        copy(a, 5, 2 * right + c, lower, to_left).start()
        copy(a, 9, 2 * right + c, lower, to_mate).start()

    def relay_rest(a):
        arrived(a, 1, 2 * left + c, lower)
        copy(a, 8, 2 * left + c, lower, to_mate).start()
        arrived(a, 4, 2 * right + c, upper)
        copy(a, 10, 2 * right + c, upper, to_mate).start()

    def relay_far(a):
        arrived(a, 2, 2 * opposite + c, upper)
        copy(a, 11, 2 * opposite + c, upper, to_mate).start()
        arrived(a, 5, 2 * opposite + c, lower)
        copy(a, 12, 2 * opposite + c, lower, to_mate).start()

    def project(a, count, chip_of):
        @pl.loop(0, count)
        def _(j):
            chunk = 2 * chip_of(j // 2) + j % 2
            pltpu.make_async_copy(land.at[a, chunk], rows_all.at[a, chunk], save.at[a]).start()
            at = pl.ds(pl.multiple_of(chunk * ROWS, ROWS), ROWS)
            x = land[a, chunk]
            if a == 0:
                for n in range(3):
                    part = dot(x, w_in[n]).astype(jnp.bfloat16)
                    heads_v[n, at, :] = part
                    if n > 0:
                        for i in range(3):
                            flipped_v[n - 1, chunk * 3 + i] = part[i * BLK : (i + 1) * BLK].T
            else:
                part = dot_nt(x, w_back[...]).astype(jnp.bfloat16)
                heads_v[3, at, :] = part

    mine = pl.ds(pl.multiple_of(own * WIDTH, WIDTH), WIDTH)
    start_own(0)
    loads = [
        pltpu.make_async_copy(hidden, land.at[0, own], load.at[0]),
        pltpu.make_async_copy(w_query.at[:, mine], w_in.at[0], load.at[1]),
        pltpu.make_async_copy(w_key.at[:, mine], w_in.at[1], load.at[2]),
        pltpu.make_async_copy(w_value.at[:, mine], w_in.at[2], load.at[3]),
        pltpu.make_async_copy(grad_out, land.at[1, own], load.at[4]),
        pltpu.make_async_copy(w_out.at[mine, :], w_back, load.at[5]),
    ]
    for item in loads:
        item.start()
    relay_near(0)
    start_own(1)
    for item in loads:
        item.wait()
    for a in range(2):
        if a == 1:
            relay_near(1)
        arrived(a, 6, 2 * y + 1 - c, both)
        project(a, 2, lambda i: y)
        relay_rest(a)
        arrived(a, 7, 2 * left + 1 - c, upper)
        arrived(a, 9, 2 * right + 1 - c, lower)
        arrived(a, 8, 2 * left + 1 - c, lower)
        arrived(a, 10, 2 * right + 1 - c, upper)
        project(a, 4, lambda i: (y + 1 + 2 * i) % 4)
        relay_far(a)
        arrived(a, 11, 2 * opposite + 1 - c, upper)
        arrived(a, 12, 2 * opposite + 1 - c, lower)
        project(a, 2, lambda i: opposite)
        first = 0 if a == 0 else 3
        count = 3 if a == 0 else 1
        pltpu.make_async_copy(
            heads_v.at[pl.ds(first, count)], heads.at[pl.ds(first, count)], save.at[2 + a]
        ).start()
        if a == 0:
            pltpu.make_async_copy(flipped_v, flipped, save.at[4]).start()
    for a in range(2):
        pltpu.make_async_copy(land.at[a], rows_all.at[a], save.at[a]).wait()
        first, count = (0, 3) if a == 0 else (3, 1)
        pltpu.make_async_copy(
            heads_v.at[pl.ds(first, count)], heads.at[pl.ds(first, count)], save.at[2 + a]
        ).wait()
        if a == 0:
            pltpu.make_async_copy(flipped_v, flipped, save.at[4]).wait()
        for slot, chunk, part in (
            (0, own, upper), (1, own, lower), (2, 2 * left + c, upper),
            (3, own, lower), (4, own, upper), (5, 2 * right + c, lower),
            (6, own, both), (7, 2 * left + c, upper), (8, 2 * left + c, lower),
            (9, 2 * right + c, lower), (10, 2 * right + c, upper),
            (11, 2 * opposite + c, upper), (12, 2 * opposite + c, lower),
        ):
            copy(a, slot, chunk, part, to_mate).wait_send()


def gather(hidden, grad_out, w_query, w_key, w_value, w_out):
    anywhere = pl.BlockSpec(memory_space=pl.ANY)
    length = CHUNKS * ROWS
    blocks = length // BLK
    bf16 = jnp.bfloat16
    return pl.pallas_call(
        gather_kernel,
        out_shape=(
            jax.ShapeDtypeStruct((2, CHUNKS, ROWS, D), bf16),
            jax.ShapeDtypeStruct((4, length, WIDTH), bf16),
            jax.ShapeDtypeStruct((2, blocks, BLK, BLK), bf16),
        ),
        in_specs=[anywhere] * 6,
        out_specs=(anywhere,) * 3,
        scratch_shapes=[
            pltpu.VMEM((2, CHUNKS, ROWS, D), bf16),
            pltpu.VMEM((3, D, WIDTH), bf16),
            pltpu.VMEM((WIDTH, D), bf16),
            pltpu.VMEM((4, length, WIDTH), bf16),
            pltpu.VMEM((2, blocks, BLK, BLK), bf16),
            pltpu.SemaphoreType.DMA((2, 13)),
            pltpu.SemaphoreType.DMA((2, 13)),
            pltpu.SemaphoreType.DMA((6,)),
            pltpu.SemaphoreType.DMA((6,)),
        ],
        compiler_params=pltpu.CompilerParams(
            collective_id=0, has_side_effects=True, vmem_limit_bytes=60 << 20
        ),
        name="gather_and_project",
    )(hidden, grad_out, w_query, w_key, w_value, w_out)


SHIFTS = ((0, 1), (1, 0), (1, 1), (3, 0), (3, 1), (2, 0), (2, 1))


def return_kernel(
    norm, rows_all, grads, flipped, w_query, w_key, w_value, grad_hidden, grad_weights,
    rows_v, flipped_v, w_v, back, out_acc, back_part, part_acc, part, x_in, z_out, z_in,
    y_send, y_recv, via, v_send, v_recv, f_send, o_send, o_recv, x_send, x_recv, z_send, z_recv, load,
):
    y, c = lax.axis_index("seq_0"), lax.axis_index("seq_1")
    x, z = lax.axis_index("batch_0"), lax.axis_index("batch_1")
    own = 2 * y + c
    peers = [dict(seq_0=(y + dy) % 4, seq_1=(c + dc) % 2) for dy, dc in SHIFTS]
    x_peers = [(x + i) % 4 for i in (1, 3, 2)]
    z_peers = [(z + i) % 8 for i in (1, 7, 2, 6, 3, 5, 4)]

    barrier = pltpu.get_barrier_semaphore()
    everyone = peers + [dict(batch_0=p) for p in x_peers] + [dict(batch_1=p) for p in z_peers]
    for peer in everyone:
        pl.semaphore_signal(barrier, inc=1, device_id=peer, device_id_type=pl.DeviceIdType.MESH)
    pl.semaphore_wait(barrier, len(everyone))

    def chunk_of(peer):
        return 2 * peer["seq_0"] + peer["seq_1"]

    def lanes(chunk):
        return pl.ds(pl.multiple_of(chunk * WIDTH, WIDTH), WIDTH)

    def rows(chunk):
        return pl.ds(pl.multiple_of(chunk * ROWS, ROWS), ROWS)

    def y_copy(a, i):
        peer = peers[i]
        return remote(
            grads.at[a, rows(chunk_of(peer))], back.at[a, :, lanes(own)],
            y_send.at[a, i], y_recv.at[a, own], **peer,
        )

    def y_wait(a, chunk):
        pltpu.make_async_remote_copy(
            src_ref=grads.at[a, rows(chunk)], dst_ref=back.at[a, :, lanes(chunk)],
            send_sem=y_send.at[a, 0], recv_sem=y_recv.at[a, chunk],
            device_id=peers[0], device_id_type=pl.DeviceIdType.MESH,
        ).wait_recv()

    beside = ((y + 1) % 4, (y + 3) % 4)

    def far_copy(a, side):
        return remote(
            grads.at[a, rows(2 * ((y + 2) % 4) + side)], via.at[side, a],
            v_send.at[a, side], v_recv.at[a, side], seq_0=beside[side], seq_1=c,
        )

    def pass_on(a, side):
        source = 2 * beside[1 - side] + c
        return remote(
            via.at[side, a], back.at[a, :, lanes(source)],
            f_send.at[a, side], y_recv.at[a, source], seq_0=beside[side], seq_1=side,
        )

    def relay(a):
        for side in range(2):
            far_copy(a, side).wait_recv()
            pass_on(a, side).start()

    loads = [
        pltpu.make_async_copy(rows_all.at[1], rows_v.at[1], load.at[0]),
        pltpu.make_async_copy(flipped, flipped_v, load.at[1]),
        pltpu.make_async_copy(rows_all.at[0], rows_v.at[0], load.at[2]),
        pltpu.make_async_copy(w_query, w_v.at[0], load.at[3]),
        pltpu.make_async_copy(w_key, w_v.at[1], load.at[4]),
        pltpu.make_async_copy(w_value, w_v.at[2], load.at[5]),
    ] + [
        pltpu.make_async_copy(grads.at[a, rows(own)], back.at[a, :, lanes(own)], load.at[6 + a])
        for a in range(3)
    ]
    for item in loads[:2]:
        item.start()
    for a in (2, 1, 0):
        for side in range(2):
            far_copy(a, side).start()
    for i in range(5):
        y_copy(2, i).start()
    for item in loads[2:]:
        item.start()

    def side_by_side(a, j):
        return jnp.concatenate([flipped_v[a, 3 * j + i] for i in range(3)], axis=1)

    loads[0].wait()
    loads[1].wait()
    part_acc[0:WIDTH] = dot(side_by_side(3, 0), rows_v[1, 0])

    @pl.loop(1, CHUNKS)
    def _(j):
        part_acc[0:WIDTH] += dot(side_by_side(3, j), rows_v[1, j])

    back_part[...] = part_acc[0:WIDTH].astype(jnp.bfloat16)

    def o_copy(i):
        peer = peers[i]
        return remote(
            back_part.at[:, lanes(chunk_of(peer))], part.at[3, lanes(own)],
            o_send.at[i], o_recv.at[own], **peer,
        )

    def o_wait(chunk):
        pltpu.make_async_remote_copy(
            src_ref=back_part.at[:, lanes(chunk)], dst_ref=part.at[3, lanes(chunk)],
            send_sem=o_send.at[0], recv_sem=o_recv.at[chunk],
            device_id=peers[0], device_id_type=pl.DeviceIdType.MESH,
        ).wait_recv()

    for i in range(7):
        o_copy(i).start()
    relay(2)
    for a in (1, 0):
        for i in range(5):
            y_copy(a, i).start()
    part[3, lanes(own), :] = back_part[:, lanes(own)]

    loads[2].wait()

    def three(j):
        return jnp.concatenate([side_by_side(a, j) for a in range(3)], axis=0)

    part_acc[...] = dot(three(0), rows_v[0, 0])

    @pl.loop(1, CHUNKS)
    def _(j):
        part_acc[...] += dot(three(j), rows_v[0, j])

    @pl.loop(0, 8)
    def _(t):
        for a in range(3):
            tile = part_acc[pl.ds(a * WIDTH, WIDTH), lanes(t)]
            part[a, lanes(t), :] = tile.T.astype(jnp.bfloat16)

    quarter = D // 4

    def x_copy(k, i):
        p = x_peers[i]
        which = pl.ds(0, 3) if k == 0 else pl.ds(3, 1)
        return remote(
            part.at[which, pl.ds(pl.multiple_of(p * quarter, quarter), quarter)],
            x_in.at[x, which], x_send.at[k, i], x_recv.at[k, x], batch_0=p,
        )

    def x_wait(k, p):
        which = pl.ds(0, 3) if k == 0 else pl.ds(3, 1)
        pltpu.make_async_remote_copy(
            src_ref=x_in.at[p, which], dst_ref=x_in.at[p, which],
            send_sem=x_send.at[k, 0], recv_sem=x_recv.at[k, p],
            device_id=dict(batch_0=x_peers[0]), device_id_type=pl.DeviceIdType.MESH,
        ).wait_recv()

    for i in range(3):
        x_copy(0, i).start()
    relay(1)
    relay(0)
    for item in loads[3:]:
        item.wait()

    def add_chips(count, chip_of, first):
        @pl.loop(0, count)
        def _(j):
            at = pl.ds(pl.multiple_of(chip_of(j) * 2 * WIDTH, 2 * WIDTH), 2 * WIDTH)
            total = dot_nt(back[0, :, at], w_v[0, :, at])
            total += dot_nt(back[1, :, at], w_v[1, :, at])
            total += dot_nt(back[2, :, at], w_v[2, :, at])
            if first:
                out_acc[...] = total
            else:
                out_acc[...] += total

    for a in (2, 1, 0):
        y_wait(a, 2 * y + 1 - c)
    add_chips(1, lambda j: y, True)

    for peer in peers:
        o_wait(chunk_of(peer))
    for i in range(3):
        x_copy(1, i).start()
    for p in x_peers:
        x_wait(0, p)
    for p in x_peers:
        x_wait(1, p)
    total = part[:, pl.ds(pl.multiple_of(x * quarter, quarter), quarter), :].astype(jnp.float32)
    for p in x_peers:
        total += x_in[p].astype(jnp.float32)
    z_out[...] = total.astype(jnp.bfloat16)

    def z_copy(i):
        p = z_peers[i]
        return remote(
            z_out.at[:, pl.ds(pl.multiple_of(p * 32, 32), 32)], z_in.at[z],
            z_send.at[i], z_recv.at[z], batch_1=p,
        )

    def z_wait(p):
        pltpu.make_async_remote_copy(
            src_ref=z_in.at[p], dst_ref=z_in.at[p],
            send_sem=z_send.at[0], recv_sem=z_recv.at[p],
            device_id=dict(batch_1=z_peers[0]), device_id_type=pl.DeviceIdType.MESH,
        ).wait_recv()

    for i in range(7):
        z_copy(i).start()

    for a in (2, 1, 0):
        for peer in peers[1:5]:
            y_wait(a, chunk_of(peer))
    add_chips(2, lambda j: (y + 1 + 2 * j) % 4, False)

    for p in z_peers:
        z_wait(p)
    total = z_out[:, pl.ds(pl.multiple_of(z * 32, 32), 32), :].astype(jnp.float32)
    for p in z_peers:
        total += z_in[p].astype(jnp.float32)
    grad_weights[...] = total * norm

    for a in (2, 1, 0):
        for peer in peers[5:]:
            y_wait(a, chunk_of(peer))
    at = pl.ds(pl.multiple_of(((y + 2) % 4) * 2 * WIDTH, 2 * WIDTH), 2 * WIDTH)
    total = dot_nt(back[0, :, at], w_v[0, :, at])
    total += dot_nt(back[1, :, at], w_v[1, :, at])
    total += dot_nt(back[2, :, at], w_v[2, :, at])
    grad_hidden[...] = (out_acc[...] + total).astype(jnp.bfloat16)

    for i in range(7):
        for a in range(3 if i < 5 else 0):
            y_copy(a, i).wait_send()
        o_copy(i).wait_send()
        z_copy(i).wait_send()
    for i in range(3):
        for k in range(2):
            x_copy(k, i).wait_send()
            far_copy(i, k).wait_send()
            pass_on(i, k).wait_send()


def hand_back(rows_all, grads, flipped, w_query, w_key, w_value, norm):
    anywhere = pl.BlockSpec(memory_space=pl.ANY)
    whole = pl.BlockSpec(memory_space=pltpu.VMEM)
    bf16 = jnp.bfloat16
    f32 = jnp.float32
    blocks = CHUNKS * ROWS // BLK
    dma = pltpu.SemaphoreType.DMA
    return pl.pallas_call(
        functools.partial(return_kernel, norm),
        out_shape=(
            jax.ShapeDtypeStruct((ROWS, D), bf16),
            jax.ShapeDtypeStruct((4, 32, WIDTH), f32),
        ),
        in_specs=[anywhere] * 6,
        out_specs=(whole, whole),
        scratch_shapes=[
            pltpu.VMEM((2, CHUNKS, ROWS, D), bf16),
            pltpu.VMEM((4, blocks, BLK, BLK), bf16),
            pltpu.VMEM((3, D, D), bf16),
            pltpu.VMEM((3, ROWS, D), bf16),
            pltpu.VMEM((ROWS, D), f32),
            pltpu.VMEM((WIDTH, D), bf16),
            pltpu.VMEM((3 * WIDTH, D), f32),
            pltpu.VMEM((4, D, WIDTH), bf16),
            pltpu.VMEM((4, 4, D // 4, WIDTH), bf16),
            pltpu.VMEM((4, D // 4, WIDTH), bf16),
            pltpu.VMEM((8, 4, 32, WIDTH), bf16),
            dma((3, 5)), dma((3, 8)), pltpu.VMEM((2, 3, ROWS, WIDTH), bf16),
            dma((3, 2)), dma((3, 2)), dma((3, 2)), dma((7,)), dma((8,)),
            dma((2, 3)), dma((2, 4)), dma((7,)), dma((8,)), dma((9,)),
        ],
        compiler_params=pltpu.CompilerParams(
            collective_id=1, has_side_effects=True, vmem_limit_bytes=60 << 20
        ),
        name="return_and_reduce",
    )(rows_all, grads, flipped, w_query, w_key, w_value)


BATCH = ("batch_0", "batch_1")
SEQ = ("seq_0", "seq_1")


def per_device(hidden, grad_out, block_offsets, w_query, w_key, w_value, w_out):
    norm = 1.0 / math.sqrt(ROWS * lax.axis_size(SEQ) * lax.axis_size(BATCH))
    rows_all, heads, turned = gather(hidden[0], grad_out[0], w_query, w_key, w_value, w_out)
    grads, flipped = attention(block_offsets[0], heads, turned)
    grad_hidden, grad_weights = hand_back(
        rows_all, grads, flipped, w_query, w_key, w_value, norm
    )
    return (grad_hidden[None], grad_weights)


def solution(mesh):
    torus = Mesh(mesh.devices.reshape(4, 2, 4, 8), ("seq_0", "seq_1", "batch_0", "batch_1"))
    in_specs = (
        P(BATCH, SEQ, None),
        P(BATCH, SEQ, None),
        P(BATCH, SEQ, None, None),
        P(),
        P(),
        P(),
        P(),
    )
    out_specs = (P(BATCH, SEQ, None), P(None, BATCH, SEQ))
    return jax.shard_map(
        per_device, mesh=torus, in_specs=in_specs, out_specs=out_specs, check_vma=False
    )
```
